128 devices in a mesh: sample: 4 (over z), marker: 32 (over y, x, core).
Axes of the slice: x: 4, y: 4, z: 4, core: 2. Of those that a mesh axis runs over, the one named last changes fastest.
Arguments:
- genotypes: bfloat16 [8192, 131072], P('sample', 'marker'), may hold values from -6 to 6
- phenotypes: float32 [16, 8192], P(None, 'sample'), may hold values from -6 to 6
- message: float32 [16, 131072], P(None, 'marker'), may hold values from -6 to 6
- probes: float32 [112, 131072], P(None, 'marker'), may hold values from -16 to 16
- inclusion: float32 [16], replicated, may hold values from 0.3 to 0.6
- slab_ratio: float32 [16], replicated, may hold values from 0.25 to 0.67
- input_precision: float32 [16], replicated, may hold values from 0.5 to 2
- noise_precision: float32 [16], replicated, may hold values from 4 to 16
Outputs:
- estimate: float32 [16, 131072], P(None, 'marker')
- lmmse_estimate: float32 [16, 131072], P(None, 'marker')
The draws below stay inside these ranges and needn't reach their ends.
All inputs are finite; a program needn't handle non-finite values.
Results may differ from the reference program's by a relative error of at most 0.0013.
Values may be sent and summed in bfloat16 or wider, within the bound.
A program may use at most 128 MiB of HBM per device.

```python
import math
import jax
import jax.numpy as jnp
from jax import lax

MARKERS = 131072
TRAITS = 16
PROBES = 7
ITERS = 2
PEOPLE = 8192


def draw_genotypes(key, part):
    block_span = 64
    blocks = MARKERS // block_span
    key_own = jax.random.fold_in(key, 21)
    key_shared = jax.random.fold_in(key, 22)
    key_strength = jax.random.fold_in(key, 23)
    key_jitter = jax.random.fold_in(key, 24)
    strength = jnp.exp(jax.random.uniform(key_strength, (1, blocks, 1), jnp.float32, math.log(0.15), math.log(0.7)))
    jitter = jax.random.uniform(key_jitter, (1, blocks, block_span), jnp.float32, 0.8, 1.2)
    sharing = strength * jitter
    shared = jax.random.truncated_normal(key_shared, -4.0, 4.0, (PEOPLE, blocks, 1), jnp.float32)
    private = jax.random.truncated_normal(key_own, -4.0, 4.0, (PEOPLE, blocks, block_span), jnp.float32)
    values = jnp.sqrt(1.0 - sharing) * private + jnp.sqrt(sharing) * shared
    return values.reshape(PEOPLE, MARKERS).astype(jnp.bfloat16)


def draw_probes(key, part):
    block_span = 64
    blocks = MARKERS // block_span
    probe_rows = PROBES * TRAITS
    key_noise = jax.random.fold_in(key, 11)
    key_factor = jax.random.fold_in(key, 12)
    key_block = jax.random.fold_in(key, 13)
    key_coherence = jax.random.fold_in(key, 14)
    key_rowscale = jax.random.fold_in(key, 15)
    position = jnp.arange(MARKERS, dtype=jnp.float32) / (MARKERS - 1.0)
    factor = jax.random.uniform(key_factor, (1, MARKERS), jnp.float32, 1.0, 2.0)
    coherence = jnp.exp(jax.random.uniform(key_coherence, (probe_rows, 1, 1), jnp.float32, math.log(0.05), math.log(4.0)))
    row_scale = jnp.exp(jax.random.uniform(key_rowscale, (probe_rows, 1), jnp.float32, math.log(0.5), math.log(2.0)))
    growth = jnp.exp(math.log(3.0) * position)[None, :]
    block_part = jax.random.truncated_normal(key_block, -4.0, 4.0, (probe_rows, blocks, 1), jnp.float32)
    noise_part = jax.random.truncated_normal(key_noise, -4.0, 4.0, (probe_rows, blocks, block_span), jnp.float32)
    blended = (coherence * block_part + noise_part) / jnp.sqrt(1.0 + coherence * coherence)
    values = blended.reshape(probe_rows, MARKERS) * row_scale * growth * factor * 0.18
    return jnp.clip(values, -16.0, 16.0).astype(jnp.float32)


def block_scale(stream_key, shape, cuts, smallest, high):
    def one(axis_at, parts):
        steps = jax.random.uniform(jax.random.fold_in(jax.random.fold_in(stream_key, 6), axis_at), (parts,), jnp.float32, smallest / len(cuts), high / len(cuts))
        return jnp.repeat(jnp.exp(steps), shape[axis_at] // parts).reshape((-1,) + (1,) * (len(shape) - axis_at - 1))

    gain = one(*cuts[0])
    for cut in cuts[1:]:
        gain = gain * one(*cut)
    return gain


def noise(stream_key, dims, scale, bound, shards=(), kind=jnp.bfloat16):
    factor_of = block_scale(stream_key, dims, shards, -0.22, 0.18) if shards else 1.0
    result = jax.random.normal(stream_key, dims, jnp.float32) * scale * factor_of
    return jnp.minimum(jnp.maximum(result, -bound), bound).astype(kind)


def setup_inputs(seed: int = 0) -> dict:
    keys = jax.random.split(jax.random.key(seed), 9)
    genotypes = draw_genotypes(jax.random.fold_in(keys[8], 71), 0)
    phenotypes = noise(keys[1], (TRAITS, PEOPLE), 1.0, 6.0, ((1, 4),), jnp.float32)
    message = noise(keys[2], (TRAITS, MARKERS), 1.0, 6.0, ((1, 32),), jnp.float32)
    probes = draw_probes(jax.random.fold_in(keys[8], 71), 0)
    inclusion = jnp.clip(jax.random.uniform(keys[4], (TRAITS,), jnp.float32, 0.3, 0.6), 0.3, 0.6)
    slab_ratio = jnp.clip(jax.random.uniform(keys[5], (TRAITS,), jnp.float32, 0.25, 0.67), 0.25, 0.67)
    input_precision = jnp.clip(jnp.exp(jax.random.uniform(keys[6], (TRAITS,), jnp.float32, math.log(0.5), math.log(2.0))), 0.5, 2.0)
    noise_precision = jnp.clip(jnp.exp(jax.random.uniform(keys[7], (TRAITS,), jnp.float32, math.log(4.0), math.log(16.0))), 4.0, 16.0)
    return dict(genotypes=genotypes, phenotypes=phenotypes, message=message, probes=probes, inclusion=inclusion, slab_ratio=slab_ratio, input_precision=input_precision, noise_precision=noise_precision)


def denoise(signal, precision, shrink, logit_base):
    energy = shrink * precision * signal * signal
    weight = jax.nn.sigmoid(logit_base + 0.5 * energy)
    return shrink * weight * signal, shrink * weight * (1.0 + (1.0 - weight) * energy)


def contract_rows(vectors, genotypes):
    return lax.dot_general(vectors, genotypes, (((1,), (1,)), ((), ())), preferred_element_type=jnp.float32)


def reference(genotypes, phenotypes, message, probes, inclusion, slab_ratio, input_precision, noise_precision):
    shrink = (slab_ratio / (1.0 + slab_ratio))[:, None]
    odds = jnp.log(inclusion / (1.0 - inclusion))[:, None]
    logit_base = odds + 0.5 * jnp.log(1.0 - shrink)
    first, slopes = denoise(message, input_precision[:, None], shrink, logit_base)
    first_slope = jnp.sum(slopes, axis=1) / MARKERS
    second_precision = input_precision * (1.0 - first_slope) / first_slope
    centre = (first - first_slope[:, None] * message) / (1.0 - first_slope)[:, None]
    centre_b = centre.astype(jnp.bfloat16)
    misfit = phenotypes - contract_rows(centre_b, genotypes)
    misfit_b = misfit.astype(jnp.bfloat16)
    start_res = (noise_precision[:, None] / PEOPLE) * jnp.dot(misfit_b, genotypes, preferred_element_type=jnp.float32)
    copies = 1 + PROBES
    scale_col = jnp.tile(noise_precision / PEOPLE, copies)[:, None]
    prec_col = jnp.tile(second_precision, copies)[:, None]
    iterate = jnp.concatenate([centre, jnp.zeros((PROBES * TRAITS, MARKERS), jnp.float32)], axis=0)
    residual = jnp.concatenate([start_res, probes], axis=0)
    direction = residual
    norm_start = jnp.sum(residual * residual, axis=1)
    norm_now = norm_start
    for iteration in range(ITERS):
        direction_b = direction.astype(jnp.bfloat16)
        predicted = contract_rows(direction_b, genotypes).astype(jnp.bfloat16)
        applied = scale_col * jnp.dot(predicted, genotypes, preferred_element_type=jnp.float32) + prec_col * direction
        step_size = norm_now / jnp.sum(direction * applied, axis=1)
        iterate = iterate + step_size[:, None] * direction
        if iteration + 1 < ITERS:
            residual = residual - step_size[:, None] * applied
            norm_next = jnp.sum(residual * residual, axis=1)
            direction = residual + (norm_next / norm_now)[:, None] * direction
            norm_now = norm_next
    lmmse_estimate = iterate[:TRAITS]
    probe_dot = jnp.sum(jnp.sum(probes * iterate[TRAITS:], axis=1).reshape(PROBES, TRAITS), axis=0)
    probe_norm = jnp.sum(norm_start[TRAITS:].reshape(PROBES, TRAITS), axis=0)
    second_slope = second_precision * probe_dot / (probe_norm + 1e-6)
    next_precision = second_precision * (1.0 - second_slope) / second_slope
    next_message = (lmmse_estimate - second_slope[:, None] * centre) / (1.0 - second_slope)[:, None]
    slab_var = slab_ratio / input_precision
    next_shrink = (slab_var * next_precision / (1.0 + slab_var * next_precision))[:, None]
    next_base = odds + 0.5 * jnp.log(1.0 - next_shrink)
    estimate, unused_slopes = denoise(next_message, next_precision[:, None], next_shrink, next_base)
    return estimate, lmmse_estimate
```

```python
import functools

import jax
import jax.numpy as jnp
from jax import lax
from jax.experimental import pallas as pl
from jax.experimental.pallas import tpu as pltpu
from jax.sharding import PartitionSpec as P

MESH = pl.DeviceIdType.MESH
F32 = jnp.float32
BF16 = jnp.bfloat16
TRAITS = 16
ROWS = 128
LANES = 128
NT = (((1,), (1,)), ((), ()))


def denoise(signal, precision, shrink, logit_base):
    energy = shrink * precision * signal * signal
    weight = jax.nn.sigmoid(logit_base + 0.5 * energy)
    return shrink * weight * signal, shrink * weight * (1.0 + (1.0 - weight) * energy)


def iota(shape, dim):
    return lax.broadcasted_iota(jnp.int32, shape, dim)


def lane_vector(ref):
    trait = iota((1, LANES), 1) % TRAITS
    value = jnp.zeros((1, LANES), F32)
    for t in range(TRAITS):
        value = jnp.where(trait == t, ref[t], value)
    return value


def to_column(row):
    shape = (TRAITS, LANES)
    picked = jnp.where(iota(shape, 0) == iota(shape, 1), jnp.broadcast_to(row, shape), 0.0)
    return jnp.sum(picked, axis=1, keepdims=True)


def to_row(column):
    shape = (TRAITS, LANES)
    picked = jnp.where(
        iota(shape, 0) == iota(shape, 1) % TRAITS, jnp.broadcast_to(column, shape), 0.0
    )
    return jnp.sum(picked, axis=0, keepdims=True)


def kernel(
    total_people,
    total_markers,
    geno_hbm,
    pheno_hbm,
    message,
    probes_hbm,
    incl,
    slab,
    in_prec,
    noise_prec,
    estimate,
    lmmse,
    geno,
    pheno,
    probes,
    centre,
    v1,
    v2,
    v3,
    slope_out,
    slope_in,
    t1_out,
    t1_in,
    t1_mine,
    t1_all,
    p1_out,
    p1_in,
    p1_mine,
    p1_all,
    t2_out,
    t2_in,
    t2_mine,
    t2_all,
    u_out,
    u_in,
    pm,
    pp,
    acc_t,
    acc_p,
    zt_part,
    zt_a1,
    zt_b1,
    zt_a2,
    zt_b2,
    r0,
    back,
    zp_part,
    zp_a1,
    zp_b1,
    zp_a2,
    zp_b2,
    n0_col,
    q1_col,
    m2_col,
    m3_col,
    mom_out,
    mom_in,
    zmom_out,
    zmom_in,
    geno_sem,
    arg_sem,
    send_t,
    send_p,
    recv_slope,
    recv_t1,
    recv_t1all,
    recv_p1,
    recv_p1all,
    recv_t2,
    recv_t2all,
    recv_u,
    recv_mom,
    zsend,
    zrecv,
):
    people, markers = geno.shape
    group = t1_in.shape[0]
    chunks = geno_sem.shape[0]
    span = people // chunks
    tiles = span // LANES
    owners = 2 * tiles
    me = lax.axis_index("marker")
    zz = lax.axis_index("sample")
    tile, half = me // 2, me % 2
    zsize = zmom_in.shape[0]

    def geno_copy(j):
        rows = pl.ds(pl.multiple_of(j * span, span), span)
        return pltpu.make_async_copy(geno_hbm.at[rows], geno.at[rows], geno_sem.at[j])

    probe_copy = pltpu.make_async_copy(probes_hbm, probes, arg_sem.at[0])
    pheno_copy = pltpu.make_async_copy(pheno_hbm, pheno, arg_sem.at[1])
    probe_copy.start()
    for j in range(chunks):
        geno_copy(j).start()
    pheno_copy.start()

    barrier = pltpu.get_barrier_semaphore()

    @pl.loop(0, group)
    def _(q):
        @pl.when(q != me)
        def _():
            pl.semaphore_signal(barrier, inc=1, device_id={"marker": q}, device_id_type=MESH)

    @pl.loop(1, zsize)
    def _(d):
        pl.semaphore_signal(
            barrier, inc=1, device_id={"sample": (zz + d) % zsize}, device_id_type=MESH
        )

    def remote(src, dst, ssem, rsem, q, axis="marker"):
        return pltpu.make_async_remote_copy(
            src_ref=src,
            dst_ref=dst,
            send_sem=ssem,
            recv_sem=rsem,
            device_id={axis: q},
            device_id_type=MESH,
        )

    def others(body):
        @pl.loop(0, group)
        def _(q):
            @pl.when(q != me)
            def _():
                body(q)

    def scatter_one(out, land, ssem, rsem, q):
        return remote(out.at[q], land.at[me], ssem.at[q], rsem.at[me], q)

    def gather_one(mine, land, ssem, rsem, q):
        return remote(mine, land.at[me], ssem.at[q], rsem.at[me], q)

    def arrivals(land, ssem, rsem):
        others(lambda q: remote(land.at[q], land.at[q], ssem.at[q], rsem.at[q], q).wait_recv())

    def drained(piece, ssem, rsem):
        others(lambda q: remote(piece, piece, ssem.at[q], rsem.at[q], q).wait_send())

    incl_row, slab_row = lane_vector(incl), lane_vector(slab)
    prec_row, noise_row = lane_vector(in_prec), lane_vector(noise_prec)
    shrink_row = slab_row / (1.0 + slab_row)
    odds_row = jnp.log(incl_row / (1.0 - incl_row))
    base_row = odds_row + 0.5 * jnp.log(1.0 - shrink_row)
    scale_row = noise_row / total_people
    shrink_c, base_c, prec_c = to_column(shrink_row), to_column(base_row), to_column(prec_row)
    scale_c = to_column(scale_row)

    width = min(512, markers)

    def columns(i):
        return pl.ds(pl.multiple_of(i * width, width), width)

    def slope_step(i, total):
        return total + denoise(message[:, columns(i)], prec_c, shrink_c, base_c)[1]

    slopes = lax.fori_loop(0, markers // width, slope_step, jnp.zeros((TRAITS, width), F32))
    slope_out[...] = to_row(jnp.sum(slopes, axis=1, keepdims=True))

    pl.semaphore_wait(barrier, group - 1 + zsize - 1)

    others(lambda q: gather_one(slope_out, slope_in, send_t, recv_slope, q).start())
    slope_in[me] = slope_out[...]

    n0_col[...] = jnp.zeros_like(n0_col)
    q1_col[...] = jnp.zeros_like(q1_col)
    m2_col[...] = jnp.zeros_like(m2_col)
    m3_col[...] = jnp.zeros_like(m3_col)
    probe_copy.wait()

    @pl.loop(0, ROWS // TRAITS - 1)
    def _(k):
        rows = pl.ds(pl.multiple_of(k * TRAITS, TRAITS), TRAITS)
        below = pl.ds(pl.multiple_of(k * TRAITS + TRAITS, TRAITS), TRAITS)

        def step(i, total):
            part = probes[rows, columns(i)]
            v1[below, columns(i)] = part.astype(BF16)
            return total + part * part

        squares = lax.fori_loop(0, markers // width, step, jnp.zeros((TRAITS, width), F32))
        n0_col[below, :] = jnp.sum(squares, axis=1, keepdims=True)

    arrivals(slope_in, send_t, recv_slope)
    slope_row = jnp.sum(slope_in[...], axis=0) / total_markers
    lam_row = prec_row * (1.0 - slope_row) / slope_row
    slope_c = to_column(slope_row)

    @pl.loop(0, markers // width)
    def _(i):
        signal = message[:, columns(i)]
        first = denoise(signal, prec_c, shrink_c, base_c)[0]
        value = (first - slope_c * signal) / (1.0 - slope_c)
        centre[:, columns(i)] = value
        v1[:TRAITS, columns(i)] = value.astype(BF16)

    drained(slope_out, send_t, recv_slope)

    def rows_of(j):
        return pl.ds(pl.multiple_of(j * span, span), span)

    def put_traits(out, value, j):
        for i in range(tiles):
            for h in range(2):
                out[j * owners + 2 * i + h] = value[
                    8 * h : 8 * h + 8, LANES * i : LANES * i + LANES
                ]

    def put_rows(out, value, j):
        for i in range(tiles):
            for h in range(2):
                out[j * owners + 2 * i + h] = value[
                    64 * h : 64 * h + 64, LANES * i : LANES * i + LANES
                ].astype(BF16)

    def scatter_chunk(j, out, land, ssem, rsem):
        @pl.loop(0, owners)
        def _(i):
            q = j * owners + i

            @pl.when(q != me)
            def _():
                scatter_one(out, land, ssem, rsem, q).start()

    @pl.loop(0, chunks)
    def _(j):
        geno_copy(j).wait()
        value = lax.dot_general(v1[...], geno[rows_of(j), :], NT, preferred_element_type=F32)
        put_traits(t1_out, value[:TRAITS], j)
        scatter_chunk(j, t1_out, t1_in, send_t, recv_t1)
        put_rows(p1_out, value, j)
        scatter_chunk(j, p1_out, p1_in, send_p, recv_p1)

    trait_rows = pl.ds(pl.multiple_of(half * 8, 8), 8)
    wide_rows = pl.ds(pl.multiple_of(half * 64, 64), 64)
    tile_cols = pl.ds(pl.multiple_of(tile * LANES, LANES), LANES)

    t1_in[me] = t1_out[me]
    p1_in[me] = p1_out[me]
    pheno_copy.wait()
    arrivals(t1_in, send_t, recv_t1)
    drained(t1_out.at[0], send_t, recv_t1)
    t1_mine[...] = pheno[trait_rows, tile_cols] - jnp.sum(t1_in[...], axis=0)
    others(lambda q: gather_one(t1_mine, t1_all, send_t, recv_t1all, q).start())
    t1_all[me] = t1_mine[...]

    def summed(land):
        def step(q, total):
            return total + land[q].astype(F32)

        return lax.fori_loop(0, group, step, jnp.zeros((64, LANES), F32))

    arrivals(p1_in, send_p, recv_p1)
    drained(p1_out.at[0], send_p, recv_p1)
    p1_mine[...] = summed(p1_in).astype(BF16)
    others(lambda q: gather_one(p1_mine, p1_all, send_p, recv_p1all, q).start())
    p1_all[me] = p1_mine[...]
    widened = p1_mine[...].astype(F32)
    q1_col[wide_rows, :] = jnp.sum(widened * widened, axis=1, keepdims=True)
    q1_col[:TRAITS, :] = jnp.zeros((TRAITS, 1), F32)

    def join_traits(land):
        @pl.loop(0, people // LANES)
        def _(t):
            cols = pl.ds(pl.multiple_of(t * LANES, LANES), LANES)
            pm[:, cols] = jnp.concatenate([land[2 * t], land[2 * t + 1]], axis=0).astype(BF16)

    def back_traits():
        zt_part[...] = jnp.dot(pm[:, :span], geno[:span, :], preferred_element_type=F32)

        @pl.loop(1, chunks)
        def _(j):
            zt_part[...] += jnp.dot(
                pm[:, rows_of(j)], geno[rows_of(j), :], preferred_element_type=F32
            )

    arrivals(t1_all, send_t, recv_t1all)
    drained(t1_mine, send_t, recv_t1all)
    join_traits(t1_all)
    back_traits()

    pair = zz + 1 - 2 * (zz % 2)
    cross = (zz + zsize - 1 + 2 * (zz % 2)) % zsize
    quarter = markers // 8
    keep_a = ((zz + 1) // 2) % 2
    keep_b = zz // 2
    last = zz % 2
    two = 2 * quarter

    def cols_at(start, size):
        return pl.ds(pl.multiple_of(start, quarter), size)

    own_a, give_a = cols_at(keep_a * two, two), cols_at((1 - keep_a) * two, two)
    own_b = cols_at(2 * two + keep_b * two, two)
    give_b = cols_at(2 * two + (1 - keep_b) * two, two)
    q_own_a = cols_at(keep_a * two + last * quarter, quarter)
    q_give_a = cols_at(keep_a * two + (1 - last) * quarter, quarter)
    q_own_b = cols_at(2 * two + keep_b * two + last * quarter, quarter)
    q_give_b = cols_at(2 * two + keep_b * two + (1 - last) * quarter, quarter)

    def zcopy(src, dst, k, q):
        return remote(src, dst, zsend.at[k], zrecv.at[k], q, "sample")

    def zphase(k, part, a1, b1, a2, b2, full):
        first = (
            zcopy(part.at[:, give_a], a1, k, pair),
            zcopy(part.at[:, give_b], b1, k + 1, cross),
        )
        second = (
            zcopy(part.at[:, q_give_a], a2, k + 2, cross),
            zcopy(part.at[:, q_give_b], b2, k + 3, pair),
        )
        third = (
            zcopy(full.at[:, q_own_a], full.at[:, q_own_a], k + 4, cross),
            zcopy(full.at[:, q_own_b], full.at[:, q_own_b], k + 5, pair),
        )
        fourth = (
            zcopy(full.at[:, own_a], full.at[:, own_a], k + 6, pair),
            zcopy(full.at[:, own_b], full.at[:, own_b], k + 7, cross),
        )
        return first, second, third, fourth

    def start(copies):
        for copy in copies:
            copy.start()

    def finish(copies):
        for copy in copies:
            copy.wait()

    def add_into(part, cols, extra):
        total = part[:, cols].astype(F32) + extra[...].astype(F32)
        part[:, cols] = total.astype(part.dtype)

    def zstep1(steps, part, a1, b1, a2, b2, full):
        finish(steps[0])
        add_into(part, own_a, a1)
        add_into(part, own_b, b1)
        start(steps[1])

    def zstep2(steps, part, a1, b1, a2, b2, full):
        finish(steps[1])
        for cols, extra in ((q_own_a, a2), (q_own_b, b2)):
            total = part[:, cols].astype(F32) + extra[...].astype(F32)
            full[:, cols] = total.astype(full.dtype)
        start(steps[2])

    def zstep3(steps):
        finish(steps[2])
        start(steps[3])

    t_args = (zt_part, zt_a1, zt_b1, zt_a2, zt_b2, r0)
    t_steps = zphase(0, *t_args)
    start(t_steps[0])

    arrivals(p1_all, send_p, recv_p1all)
    drained(p1_mine, send_p, recv_p1all)

    @pl.loop(0, people // LANES)
    def _(t):
        cols = pl.ds(pl.multiple_of(t * LANES, LANES), LANES)
        pp[:64, cols] = p1_all[2 * t]
        pp[64:, cols] = p1_all[2 * t + 1]

    acc_p[...] = jnp.zeros_like(acc_p)

    def back_probes(lo, hi):
        @pl.loop(lo, hi)
        def _(j):
            acc_p[...] += jnp.dot(
                pp[:, rows_of(j)], geno[rows_of(j), :], preferred_element_type=F32
            )

    mid = (chunks + 1) // 2
    back_probes(0, mid)
    zstep1(t_steps, *t_args)
    back_probes(mid, chunks)

    @pl.loop(0, markers // width)
    def _(i):
        zp_part[:, columns(i)] = acc_p[TRAITS:, columns(i)].astype(BF16)

    zstep2(t_steps, *t_args)
    v3p = v3.at[pl.ds(TRAITS, ROWS - TRAITS)]
    p_args = (zp_part, zp_a1, zp_b1, zp_a2, zp_b2, v3p)
    p_steps = zphase(8, *p_args)
    zstep3(t_steps)
    start(p_steps[0])
    finish(t_steps[3])

    def residual_step(i, total):
        value = scale_c * r0[:, columns(i)]
        centre_free = value
        v2[:, columns(i)] = centre_free.astype(BF16)
        return total + value * value

    squares = lax.fori_loop(0, markers // width, residual_step, jnp.zeros((TRAITS, width), F32))
    n0_col[:TRAITS, :] = jnp.sum(squares, axis=1, keepdims=True)

    def second_project(lo, hi):
        @pl.loop(lo, hi)
        def _(j):
            value = lax.dot_general(v2[...], geno[rows_of(j), :], NT, preferred_element_type=F32)
            put_traits(t2_out, value, j)
            scatter_chunk(j, t2_out, t2_in, send_t, recv_t2)

    second_project(0, chunks)
    zstep1(p_steps, *p_args)
    t2_in[me] = t2_out[me]
    arrivals(t2_in, send_t, recv_t2)
    drained(t2_out.at[0], send_t, recv_t2)
    rounded = jnp.sum(t2_in[...], axis=0).astype(BF16).astype(F32)
    t2_mine[...] = rounded
    others(lambda q: gather_one(t2_mine, t2_all, send_t, recv_t2all, q).start())
    t2_all[me] = t2_mine[...]
    q1_col[trait_rows, :] = jnp.sum(rounded * rounded, axis=1, keepdims=True)
    zstep2(p_steps, *p_args)
    arrivals(t2_all, send_t, recv_t2all)
    drained(t2_mine, send_t, recv_t2all)
    join_traits(t2_all)
    back_traits2 = (acc_t, zt_a1, zt_b1, zt_a2, zt_b2, back)

    acc_t[...] = jnp.dot(pm[:, :span], geno[:span, :], preferred_element_type=F32)

    @pl.loop(1, chunks)
    def _(j):
        acc_t[...] += jnp.dot(pm[:, rows_of(j)], geno[rows_of(j), :], preferred_element_type=F32)

    s_steps = zphase(16, *back_traits2)
    start(s_steps[0])
    zstep3(p_steps)
    zstep1(s_steps, *back_traits2)
    zstep2(s_steps, *back_traits2)
    zstep3(s_steps)
    finish(p_steps[3])
    finish(s_steps[3])

    @pl.loop(0, markers // width)
    def _(i):
        v3[:TRAITS, columns(i)] = back[:, columns(i)].astype(BF16)

    @pl.loop(0, chunks)
    def _(j):
        value = lax.dot_general(v3[...], geno[rows_of(j), :], NT, preferred_element_type=F32)
        put_rows(u_out, value, j)
        scatter_chunk(j, u_out, u_in, send_p, recv_u)

    u_in[me] = u_out[me]
    arrivals(u_in, send_p, recv_u)
    drained(u_out.at[0], send_p, recv_u)
    u = summed(u_in)
    mine = p1_mine[...].astype(F32)
    top = jnp.concatenate([t2_all[2 * tile], t2_all[2 * tile + 1]], axis=0)
    mine = jnp.concatenate([jnp.where(half == 0, top, mine[:TRAITS]), mine[TRAITS:]], axis=0)
    m2_col[wide_rows, :] = jnp.sum(u * mine, axis=1, keepdims=True)
    m3_col[wide_rows, :] = jnp.sum(u * u, axis=1, keepdims=True)

    lane = iota((ROWS, LANES), 1)
    moments = jnp.where(lane == 0, n0_col[...] * (1.0 / zsize), 0.0)
    moments = jnp.where(lane == 1, q1_col[...], moments)
    moments = jnp.where(lane == 2, m2_col[...], moments)
    moments = jnp.where(lane == 3, m3_col[...], moments)
    mom_out[...] = jnp.transpose(moments)[:8]
    others(lambda q: gather_one(mom_out, mom_in, send_t, recv_mom, q).start())
    mom_in[me] = mom_out[...]
    arrivals(mom_in, send_t, recv_mom)
    drained(mom_out, send_t, recv_mom)
    zmom_out[...] = jnp.sum(mom_in[...], axis=0)

    def zmom(d):
        q = (zz + d) % zsize
        return zcopy(zmom_out, zmom_in.at[d], 24 + d, q)

    for d in range(1, zsize):
        zmom(d).start()
    zmom_in[0] = zmom_out[...]
    for d in range(1, zsize):
        zmom(d).wait()
    totals = jnp.zeros((8, LANES), F32)
    for q in range(zsize):
        totals = totals + zmom_in[(zz + zsize - q) % zsize]

    n0, q1, m2, m3 = totals[0:1], totals[1:2], totals[2:3], totals[3:4]
    step1 = n0 / (scale_row * q1 + lam_row * n0)
    shrunk = 1.0 - step1 * lam_row
    gain = step1 * scale_row
    n1 = shrunk * shrunk * n0 - 2.0 * shrunk * gain * q1 + gain * gain * m2
    beta = n1 / n0
    mix = shrunk + beta
    p2 = mix * mix * q1 - 2.0 * mix * gain * m2 + gain * gain * m3
    step2 = n1 / (scale_row * p2 + lam_row * (n1 + beta * beta * n0))
    is_probe = iota((1, LANES), 1) >= TRAITS
    dot_row = jnp.where(is_probe, step1 * n0 + step2 * n1, 0.0)
    norm_row = jnp.where(is_probe, n0, 0.0)
    for shift in (16, 32, 64):
        dot_row = dot_row + pltpu.roll(dot_row, shift, 1)
        norm_row = norm_row + pltpu.roll(norm_row, shift, 1)
    eta = lam_row * dot_row / (norm_row + 1e-6)
    next_prec = lam_row * (1.0 - eta) / eta
    slab_var = slab_row / prec_row
    next_shrink = slab_var * next_prec / (1.0 + slab_var * next_prec)
    next_base = odds_row + 0.5 * jnp.log(1.0 - next_shrink)

    along_r = to_column((step1 + step2 * mix) * scale_row)
    along_b = to_column(step2 * gain)
    eta_c, prec2_c = to_column(eta), to_column(next_prec)
    shrink2_c, base2_c = to_column(next_shrink), to_column(next_base)

    @pl.loop(0, markers // width)
    def _(i):
        middle = centre[:, columns(i)]
        found = middle + along_r * r0[:, columns(i)] - along_b * back[:, columns(i)]
        lmmse[:, columns(i)] = found
        signal = (found - eta_c * middle) / (1.0 - eta_c)
        estimate[:, columns(i)] = denoise(signal, prec2_c, shrink2_c, base2_c)[0]


def per_device(
    genotypes, phenotypes, message, probes, inclusion, slab_ratio, input_precision, noise_precision
):
    people, markers = genotypes.shape
    zsize, group = lax.axis_size("sample"), lax.axis_size("marker")
    assert group == 2 * people // LANES and zsize == 4
    assert message.shape[0] == TRAITS and probes.shape[0] == ROWS - TRAITS
    chunks = max(1, people // 512)
    rest = ROWS - TRAITS
    quarter = markers // 8
    vmem = pltpu.VMEM
    dma = pltpu.SemaphoreType.DMA
    piece_t = vmem((group, 8, LANES), F32)
    piece_p = vmem((group, 64, LANES), BF16)
    whole = pl.BlockSpec(memory_space=pltpu.VMEM)
    far = pl.BlockSpec(memory_space=pl.ANY)
    scalars = pl.BlockSpec(memory_space=pltpu.SMEM)
    out = jax.ShapeDtypeStruct((TRAITS, markers), F32)
    return pl.pallas_call(
        functools.partial(kernel, float(people * zsize), float(markers * group)),
        out_shape=(out, out),
        in_specs=[far, far, whole, far, scalars, scalars, scalars, scalars],
        out_specs=(whole, whole),
        scratch_shapes=[
            vmem((people, markers), BF16),
            vmem((TRAITS, people), F32),
            vmem((rest, markers), F32),
            vmem((TRAITS, markers), F32),
            vmem((ROWS, markers), BF16),
            vmem((TRAITS, markers), BF16),
            vmem((ROWS, markers), BF16),
            vmem((1, LANES), F32),
            vmem((group, 1, LANES), F32),
            piece_t,
            piece_t,
            vmem((8, LANES), F32),
            piece_t,
            piece_p,
            piece_p,
            vmem((64, LANES), BF16),
            piece_p,
            piece_t,
            piece_t,
            vmem((8, LANES), F32),
            piece_t,
            piece_p,
            piece_p,
            vmem((TRAITS, people), BF16),
            vmem((ROWS, people), BF16),
            vmem((TRAITS, markers), F32),
            vmem((ROWS, markers), F32),
            vmem((TRAITS, markers), F32),
            vmem((TRAITS, 2 * quarter), F32),
            vmem((TRAITS, 2 * quarter), F32),
            vmem((TRAITS, quarter), F32),
            vmem((TRAITS, quarter), F32),
            vmem((TRAITS, markers), F32),
            vmem((TRAITS, markers), F32),
            vmem((rest, markers), BF16),
            vmem((rest, 2 * quarter), BF16),
            vmem((rest, 2 * quarter), BF16),
            vmem((rest, quarter), BF16),
            vmem((rest, quarter), BF16),
            vmem((ROWS, 1), F32),
            vmem((ROWS, 1), F32),
            vmem((ROWS, 1), F32),
            vmem((ROWS, 1), F32),
            vmem((8, LANES), F32),
            vmem((group, 8, LANES), F32),
            vmem((8, LANES), F32),
            vmem((zsize, 8, LANES), F32),
            dma((chunks,)),
            dma((2,)),
            dma((group,)),
            dma((group,)),
            dma((group,)),
            dma((group,)),
            dma((group,)),
            dma((group,)),
            dma((group,)),
            dma((group,)),
            dma((group,)),
            dma((group,)),
            dma((group,)),
            dma((24 + zsize,)),
            dma((24 + zsize,)),
        ],
        compiler_params=pltpu.CompilerParams(
            collective_id=0, has_side_effects=True, vmem_limit_bytes=60 << 20
        ),
        name="vamp_round",
    )(
        genotypes,
        phenotypes,
        message,
        probes,
        inclusion,
        slab_ratio,
        input_precision,
        noise_precision,
    )


def solution(mesh):
    return jax.shard_map(
        per_device,
        mesh=mesh,
        in_specs=(
            P("sample", "marker"),
            P(None, "sample"),
            P(None, "marker"),
            P(None, "marker"),
            P(),
            P(),
            P(),
            P(),
        ),
        out_specs=(P(None, "marker"), P(None, "marker")),
        check_vma=False,
    )
```

```python
import functools

import jax
import jax.numpy as jnp
from jax import lax
from jax.experimental import pallas as pl
from jax.experimental.pallas import tpu as pltpu
from jax.sharding import PartitionSpec as P

MESH = pl.DeviceIdType.MESH
F32 = jnp.float32
BF16 = jnp.bfloat16
TRAITS = 16
ROWS = 128
LANES = 128
NT = (((1,), (1,)), ((), ()))


def denoise(signal, precision, shrink, logit_base):
    energy = shrink * precision * signal * signal
    weight = jax.nn.sigmoid(logit_base + 0.5 * energy)
    return shrink * weight * signal, shrink * weight * (1.0 + (1.0 - weight) * energy)


def iota(shape, dim):
    return lax.broadcasted_iota(jnp.int32, shape, dim)


def lane_vector(ref):
    trait = iota((1, LANES), 1) % TRAITS
    value = jnp.zeros((1, LANES), F32)
    for t in range(TRAITS):
        value = jnp.where(trait == t, ref[t], value)
    return value


def to_column(row):
    shape = (TRAITS, LANES)
    picked = jnp.where(iota(shape, 0) == iota(shape, 1), jnp.broadcast_to(row, shape), 0.0)
    return jnp.sum(picked, axis=1, keepdims=True)


def to_row(column):
    shape = (TRAITS, LANES)
    picked = jnp.where(
        iota(shape, 0) == iota(shape, 1) % TRAITS, jnp.broadcast_to(column, shape), 0.0
    )
    return jnp.sum(picked, axis=0, keepdims=True)


def kernel(
    total_people,
    total_markers,
    geno_hbm,
    pheno_hbm,
    message_hbm,
    probes_hbm,
    incl,
    slab,
    in_prec,
    noise_prec,
    centre,
    r0,
    back,
    coefs,
    geno,
    pheno,
    message,
    probes,
    v1,
    v2,
    v3,
    slope_out,
    slope_in,
    raw,
    t1_out,
    t1_in,
    t1_mine,
    t1_all,
    p1_out,
    p1_in,
    p1_mine,
    p1_all,
    t2_out,
    t2_in,
    t2_mine,
    t2_all,
    u_out,
    u_in,
    pm,
    pp,
    acc_p,
    exact,
    exact_in1,
    exact_mid,
    exact_in2,
    zt,
    zs,
    zp_part,
    zp_a1,
    zp_b1,
    zp_a2,
    zp_b2,
    n0_col,
    q1_col,
    m2_col,
    m3_col,
    mom_out,
    mom_in,
    zmom_out,
    zmom_in,
    geno_sem,
    arg_sem,
    send_sem,
    recv_sem,
    t1_sem,
    t2_sem,
    zsend,
    zrecv,
):
    people, markers = geno.shape
    group = t1_in.shape[0]
    chunks = geno_sem.shape[0]
    span = people // chunks
    tiles = span // LANES
    owners = 2 * tiles
    me = lax.axis_index("marker")
    zz = lax.axis_index("sample")
    tile, half = me // 2, me % 2
    zsize = zmom_in.shape[0]
    SLOPE, T1, P1, T1ALL, P1ALL, T2, T2ALL, U, MOM = range(9)

    def geno_copy(j):
        rows = pl.ds(pl.multiple_of(j * span, span), span)
        return pltpu.make_async_copy(geno_hbm.at[rows], geno.at[rows], geno_sem.at[j])

    message_copy = pltpu.make_async_copy(message_hbm, message, arg_sem.at[2])
    probe_copy = pltpu.make_async_copy(probes_hbm, probes, arg_sem.at[0])
    pheno_copy = pltpu.make_async_copy(pheno_hbm, pheno, arg_sem.at[1])
    message_copy.start()
    probe_copy.start()
    for j in range(chunks):
        geno_copy(j).start()
    pheno_copy.start()

    barrier = pltpu.get_barrier_semaphore()

    @pl.loop(0, group)
    def _(q):
        @pl.when(q != me)
        def _():
            pl.semaphore_signal(barrier, inc=1, device_id={"marker": q}, device_id_type=MESH)

    @pl.loop(1, zsize)
    def _(d):
        pl.semaphore_signal(
            barrier, inc=1, device_id={"sample": (zz + d) % zsize}, device_id_type=MESH
        )

    def remote(src, dst, ssem, rsem, q, axis="marker"):
        return pltpu.make_async_remote_copy(
            src_ref=src,
            dst_ref=dst,
            send_sem=ssem,
            recv_sem=rsem,
            device_id={axis: q},
            device_id_type=MESH,
        )

    def others(body):
        @pl.loop(0, group)
        def _(q):
            @pl.when(q != me)
            def _():
                body(q)

    def scatter_one(k, out, land, q):
        return remote(out.at[q], land.at[me], send_sem.at[k], recv_sem.at[k], q)

    def gather_all(k, mine, land, sem=None):
        sem = recv_sem.at[k] if sem is None else sem
        others(lambda q: remote(mine, land.at[me], send_sem.at[k], sem, q).start())

    def bulk(k, land, count, sem=None):
        part = land.at[pl.ds(0, count)]
        sem = recv_sem.at[k] if sem is None else sem
        return remote(part, part, send_sem.at[k], sem, (me + 1) % group)

    def arrived(k, land):
        bulk(k, land, group - 1).wait_recv()

    def drained(k, land):
        bulk(k, land, group - 1).wait_send()

    incl_row, slab_row = lane_vector(incl), lane_vector(slab)
    prec_row, noise_row = lane_vector(in_prec), lane_vector(noise_prec)
    shrink_row = slab_row / (1.0 + slab_row)
    odds_row = jnp.log(incl_row / (1.0 - incl_row))
    base_row = odds_row + 0.5 * jnp.log(1.0 - shrink_row)
    scale_row = noise_row / total_people
    shrink_c, base_c, prec_c = to_column(shrink_row), to_column(base_row), to_column(prec_row)
    scale_c = to_column(scale_row)

    width = min(512, markers)
    steps = markers // width

    def columns(i):
        return pl.ds(pl.multiple_of(i * width, width), width)

    def split(rows, i, value):
        high = value.astype(BF16)
        v1[rows : rows + TRAITS, columns(i)] = high
        v1[rows + TRAITS : rows + 2 * TRAITS, columns(i)] = (value - high.astype(F32)).astype(BF16)

    def slope_step(i, total):
        signal = message[:, columns(i)]
        first, slope = denoise(signal, prec_c, shrink_c, base_c)
        centre[:, columns(i)] = first
        split(0, i, first)
        split(2 * TRAITS, i, signal)
        return total + slope

    message_copy.wait()
    slopes = lax.fori_loop(0, steps, slope_step, jnp.zeros((TRAITS, width), F32))
    slope_out[...] = to_row(jnp.sum(slopes, axis=1, keepdims=True))

    pl.semaphore_wait(barrier, group - 1 + zsize - 1)

    gather_all(SLOPE, slope_out, slope_in)
    slope_in[me] = slope_out[...]

    n0_col[...] = jnp.zeros_like(n0_col)
    q1_col[...] = jnp.zeros_like(q1_col)
    m2_col[...] = jnp.zeros_like(m2_col)
    m3_col[...] = jnp.zeros_like(m3_col)
    probe_copy.wait()

    @pl.loop(0, ROWS // TRAITS - 1)
    def _(k):
        rows = pl.ds(pl.multiple_of(k * TRAITS, TRAITS), TRAITS)
        below = pl.ds(pl.multiple_of(k * TRAITS + TRAITS, TRAITS), TRAITS)
        stacked = pl.ds(pl.multiple_of(k * TRAITS + 4 * TRAITS, TRAITS), TRAITS)

        def step(i, total):
            part = probes[rows, columns(i)]
            v1[stacked, columns(i)] = part.astype(BF16)
            return total + part * part

        squares = lax.fori_loop(0, steps, step, jnp.zeros((TRAITS, width), F32))
        n0_col[below, :] = jnp.sum(squares, axis=1, keepdims=True)

    def rows_of(j):
        return pl.ds(pl.multiple_of(j * span, span), span)

    def put_traits(out, value, j):
        for i in range(tiles):
            for h in range(2):
                out[j * owners + 2 * i + h] = value[
                    8 * h : 8 * h + 8, LANES * i : LANES * i + LANES
                ]

    def put_rows(out, value, j):
        for i in range(tiles):
            for h in range(2):
                out[j * owners + 2 * i + h] = value[
                    64 * h : 64 * h + 64, LANES * i : LANES * i + LANES
                ].astype(BF16)

    def scatter_chunk(k, j, out, land):
        @pl.loop(0, owners)
        def _(i):
            q = j * owners + i

            @pl.when(q != me)
            def _():
                scatter_one(k, out, land, q).start()

    @pl.loop(0, chunks)
    def _(j):
        geno_copy(j).wait()
        value = lax.dot_general(v1[...], geno[rows_of(j), :], NT, preferred_element_type=F32)
        raw[:, rows_of(j)] = value[: 4 * TRAITS]
        put_rows(p1_out, value[3 * TRAITS :], j)
        scatter_chunk(P1, j, p1_out, p1_in)

    arrived(SLOPE, slope_in)
    slope_row = jnp.sum(slope_in[...], axis=0) / total_markers
    lam_row = prec_row * (1.0 - slope_row) / slope_row
    slope_c = to_column(slope_row)

    @pl.loop(0, chunks)
    def _(j):
        part = raw[:, rows_of(j)]
        first = part[:TRAITS] + part[TRAITS : 2 * TRAITS]
        signal = part[2 * TRAITS : 3 * TRAITS] + part[3 * TRAITS :]
        put_traits(t1_out, (first - slope_c * signal) / (1.0 - slope_c), j)
        scatter_chunk(T1, j, t1_out, t1_in)

    drained(SLOPE, slope_in)
    trait_rows = pl.ds(pl.multiple_of(half * 8, 8), 8)
    wide_rows = pl.ds(pl.multiple_of(half * 64, 64), 64)
    tile_cols = pl.ds(pl.multiple_of(tile * LANES, LANES), LANES)

    @pl.loop(0, steps)
    def _(i):
        centre[:, columns(i)] = (centre[:, columns(i)] - slope_c * message[:, columns(i)]) / (
            1.0 - slope_c
        )

    t1_in[me] = t1_out[me]
    p1_in[me] = p1_out[me]
    pheno_copy.wait()

    arrived(T1, t1_in)
    t1_mine[...] = (pheno[trait_rows, tile_cols] - jnp.sum(t1_in[...], axis=0)).astype(BF16)
    gather_all(T1ALL, t1_mine, t1_all, t1_sem.at[me // owners])
    t1_all[me] = t1_mine[...]

    def summed(land):
        def step(q, total):
            return total + land[q].astype(F32)

        return lax.fori_loop(0, group, step, jnp.zeros((64, LANES), F32))

    arrived(P1, p1_in)
    p1_mine[...] = summed(p1_in).astype(BF16)
    gather_all(P1ALL, p1_mine, p1_all)
    p1_all[me] = p1_mine[...]
    widened = p1_mine[...].astype(F32)
    q1_col[wide_rows, :] = jnp.sum(widened * widened, axis=1, keepdims=True)
    q1_col[:TRAITS, :] = jnp.zeros((TRAITS, 1), F32)
    drained(T1, t1_in)
    drained(P1, p1_in)

    def back_traits(k, land, sems, rows):
        @pl.loop(0, chunks)
        def _(j):
            mine = me // owners == j

            @pl.when(mine)
            def _():
                bulk(k, land, owners - 1, sems.at[j]).wait_recv()

            @pl.when(jnp.logical_not(mine))
            def _():
                bulk(k, land, owners, sems.at[j]).wait_recv()

            @pl.loop(0, tiles)
            def _(i):
                t = j * tiles + i
                cols = pl.ds(pl.multiple_of(t * LANES, LANES), LANES)
                pm[:8, cols] = land[2 * t]
                pm[8:, cols] = land[2 * t + 1]

            part = jnp.dot(pm[:, rows_of(j)], geno[rows_of(j), :], preferred_element_type=F32)

            @pl.when(j == 0)
            def _():
                exact[rows, :] = part

            @pl.when(j > 0)
            def _():
                exact[rows, :] += part

        drained(k, land)

    top, low = pl.ds(0, TRAITS), pl.ds(TRAITS, TRAITS)
    back_traits(T1ALL, t1_all, t1_sem, top)

    pair = zz + 1 - 2 * (zz % 2)
    cross = (zz + zsize - 1 + 2 * (zz % 2)) % zsize
    quarter = markers // 8
    two = 2 * quarter

    def zcopy(src, dst, k, q):
        return remote(src, dst, zsend.at[k], zrecv.at[k], q, "sample")

    def start(copies):
        for copy in copies:
            copy.start()

    def finish(copies):
        for copy in copies:
            copy.wait()

    left, right = pl.ds(0, markers // 2), pl.ds(markers // 2, markers // 2)

    def doubling(k, out1, in1, out2, in2):
        return (
            (
                zcopy(out1.at[:, left], in1.at[:, left], k, pair),
                zcopy(out1.at[:, right], in1.at[:, right], k + 1, cross),
            ),
            (
                zcopy(out2.at[:, left], in2.at[:, left], k + 2, cross),
                zcopy(out2.at[:, right], in2.at[:, right], k + 3, pair),
            ),
        )

    def rounded_start(hops, z, rows):
        z[0] = exact[rows, :].astype(BF16)
        start(hops[0])

    def rounded_middle(hops, z):
        finish(hops[0])
        z[2] = (z[0].astype(F32) + z[1].astype(F32)).astype(BF16)
        start(hops[1])

    t_hops = doubling(0, zt.at[0], zt.at[1], zt.at[2], zt.at[3])
    s_hops = doubling(4, zs.at[0], zs.at[1], zs.at[2], zs.at[3])
    e_hops = doubling(8, exact, exact_in1, exact_mid, exact_in2)
    rounded_start(t_hops, zt, top)

    keep_a = ((zz + 1) // 2) % 2
    keep_b = zz // 2
    last = zz % 2

    def cols_at(start_at, size):
        return pl.ds(pl.multiple_of(start_at, quarter), size)

    own_a, give_a = cols_at(keep_a * two, two), cols_at((1 - keep_a) * two, two)
    own_b = cols_at(2 * two + keep_b * two, two)
    give_b = cols_at(2 * two + (1 - keep_b) * two, two)
    q_own_a = cols_at(keep_a * two + last * quarter, quarter)
    q_give_a = cols_at(keep_a * two + (1 - last) * quarter, quarter)
    q_own_b = cols_at(2 * two + keep_b * two + last * quarter, quarter)
    q_give_b = cols_at(2 * two + keep_b * two + (1 - last) * quarter, quarter)
    full = v3.at[pl.ds(TRAITS, ROWS - TRAITS)]
    p_hops = (
        (
            zcopy(zp_part.at[:, give_a], zp_a1, 12, pair),
            zcopy(zp_part.at[:, give_b], zp_b1, 13, cross),
        ),
        (
            zcopy(zp_part.at[:, q_give_a], zp_a2, 14, cross),
            zcopy(zp_part.at[:, q_give_b], zp_b2, 15, pair),
        ),
        (
            zcopy(full.at[:, q_own_a], full.at[:, q_own_a], 16, cross),
            zcopy(full.at[:, q_own_b], full.at[:, q_own_b], 17, pair),
        ),
        (
            zcopy(full.at[:, own_a], full.at[:, own_a], 18, pair),
            zcopy(full.at[:, own_b], full.at[:, own_b], 19, cross),
        ),
    )

    def add_into(target, cols, extra):
        total = zp_part[:, cols].astype(F32) + extra[...].astype(F32)
        target[:, cols] = total.astype(BF16)

    def probes_hop1():
        finish(p_hops[0])
        add_into(zp_part, own_a, zp_a1)
        add_into(zp_part, own_b, zp_b1)
        start(p_hops[1])

    def probes_hop2():
        finish(p_hops[1])
        add_into(full, q_own_a, zp_a2)
        add_into(full, q_own_b, zp_b2)
        start(p_hops[2])

    def probes_hop3():
        finish(p_hops[2])
        start(p_hops[3])

    arrived(P1ALL, p1_all)
    drained(P1ALL, p1_all)

    @pl.loop(0, people // LANES)
    def _(t):
        cols = pl.ds(pl.multiple_of(t * LANES, LANES), LANES)
        pp[:64, cols] = p1_all[2 * t]
        pp[64:, cols] = p1_all[2 * t + 1]

    acc_p[...] = jnp.zeros_like(acc_p)

    def back_probes(lo, hi):
        @pl.loop(lo, hi)
        def _(j):
            acc_p[...] += jnp.dot(
                pp[:, rows_of(j)], geno[rows_of(j), :], preferred_element_type=F32
            )

    mid = (chunks + 1) // 2
    back_probes(0, mid)

    rounded_middle(t_hops, zt)

    back_probes(mid, chunks)

    @pl.loop(0, steps)
    def _(i):
        zp_part[:, columns(i)] = acc_p[TRAITS:, columns(i)].astype(BF16)

    finish(t_hops[1])
    start(p_hops[0])

    def residual_step(i, total):
        cols = columns(i)
        value = scale_c * (zt[2, :, cols].astype(F32) + zt[3, :, cols].astype(F32))
        v2[:, cols] = value.astype(BF16)
        return total + value * value

    squares = lax.fori_loop(0, steps, residual_step, jnp.zeros((TRAITS, width), F32))
    n0_col[:TRAITS, :] = jnp.sum(squares, axis=1, keepdims=True)

    @pl.loop(0, chunks)
    def _(j):
        value = lax.dot_general(v2[...], geno[rows_of(j), :], NT, preferred_element_type=F32)
        put_traits(t2_out, value, j)
        scatter_chunk(T2, j, t2_out, t2_in)

    probes_hop1()
    t2_in[me] = t2_out[me]

    arrived(T2, t2_in)
    t2_mine[...] = jnp.sum(t2_in[...], axis=0).astype(BF16)
    gather_all(T2ALL, t2_mine, t2_all, t2_sem.at[me // owners])
    t2_all[me] = t2_mine[...]
    rounded = t2_mine[...].astype(F32)
    q1_col[trait_rows, :] = jnp.sum(rounded * rounded, axis=1, keepdims=True)
    drained(T2, t2_in)

    probes_hop2()

    back_traits(T2ALL, t2_all, t2_sem, low)
    rounded_start(s_hops, zs, low)

    probes_hop3()

    rounded_middle(s_hops, zs)

    finish(p_hops[3])

    finish(s_hops[1])
    start(e_hops[0])

    @pl.loop(0, steps)
    def _(i):
        cols = columns(i)
        v3[:TRAITS, cols] = (zs[2, :, cols].astype(F32) + zs[3, :, cols].astype(F32)).astype(BF16)

    @pl.loop(0, chunks)
    def _(j):
        value = lax.dot_general(v3[...], geno[rows_of(j), :], NT, preferred_element_type=F32)
        put_rows(u_out, value, j)
        scatter_chunk(U, j, u_out, u_in)

    u_in[me] = u_out[me]

    finish(e_hops[0])

    @pl.loop(0, steps)
    def _(i):
        exact_mid[:, columns(i)] = exact[:, columns(i)] + exact_in1[:, columns(i)]

    start(e_hops[1])

    arrived(U, u_in)
    u = summed(u_in)
    mine = p1_mine[...].astype(F32)
    pieces = jnp.concatenate([t2_all[2 * tile], t2_all[2 * tile + 1]], axis=0).astype(F32)
    mine = jnp.concatenate([jnp.where(half == 0, pieces, mine[:TRAITS]), mine[TRAITS:]], axis=0)
    m2_col[wide_rows, :] = jnp.sum(u * mine, axis=1, keepdims=True)
    m3_col[wide_rows, :] = jnp.sum(u * u, axis=1, keepdims=True)

    lane = iota((ROWS, LANES), 1)
    moments = jnp.where(lane == 0, n0_col[...] * (1.0 / zsize), 0.0)
    moments = jnp.where(lane == 1, q1_col[...], moments)
    moments = jnp.where(lane == 2, m2_col[...], moments)
    moments = jnp.where(lane == 3, m3_col[...], moments)
    mom_out[...] = jnp.transpose(moments)[:4]
    gather_all(MOM, mom_out, mom_in)
    mom_in[me] = mom_out[...]
    drained(U, u_in)

    finish(e_hops[1])

    @pl.loop(0, steps)
    def _(i):
        cols = columns(i)
        r0[:, cols] = scale_c * (exact_mid[:TRAITS, cols] + exact_in2[:TRAITS, cols])
        back[:, cols] = exact_mid[TRAITS:, cols] + exact_in2[TRAITS:, cols]

    arrived(MOM, mom_in)
    zmom_out[...] = jnp.sum(mom_in[...], axis=0)

    def zmom(d):
        q = (zz + d) % zsize
        return zcopy(zmom_out, zmom_in.at[d], 19 + d, q)

    for d in range(1, zsize):
        zmom(d).start()
    zmom_in[0] = zmom_out[...]
    drained(MOM, mom_in)
    for d in range(1, zsize):
        zmom(d).wait()
    totals = jnp.zeros((4, LANES), F32)
    for q in range(zsize):
        totals = totals + zmom_in[(zz + zsize - q) % zsize]

    n0, q1, m2, m3 = totals[0:1], totals[1:2], totals[2:3], totals[3:4]
    step1 = n0 / (scale_row * q1 + lam_row * n0)
    shrunk = 1.0 - step1 * lam_row
    gain = step1 * scale_row
    n1 = shrunk * shrunk * n0 - 2.0 * shrunk * gain * q1 + gain * gain * m2
    beta = n1 / n0
    mix = shrunk + beta
    p2 = mix * mix * q1 - 2.0 * mix * gain * m2 + gain * gain * m3
    step2 = n1 / (scale_row * p2 + lam_row * (n1 + beta * beta * n0))
    is_probe = iota((1, LANES), 1) >= TRAITS
    dot_row = jnp.where(is_probe, step1 * n0 + step2 * n1, 0.0)
    norm_row = jnp.where(is_probe, n0, 0.0)
    for shift in (16, 32, 64):
        dot_row = dot_row + pltpu.roll(dot_row, shift, 1)
        norm_row = norm_row + pltpu.roll(norm_row, shift, 1)
    eta = lam_row * dot_row / (norm_row + 1e-6)
    next_prec = lam_row * (1.0 - eta) / eta
    slab_var = slab_row / prec_row
    next_shrink = slab_var * next_prec / (1.0 + slab_var * next_prec)
    next_base = odds_row + 0.5 * jnp.log(1.0 - next_shrink)
    lane = iota((TRAITS, LANES), 1)
    table = jnp.zeros((TRAITS, LANES), F32)
    for k, row in enumerate(
        (step1 + step2 * mix, step2 * gain, eta, next_prec, next_shrink, next_base)
    ):
        table = jnp.where(lane == k, to_column(row), table)
    coefs[...] = table


def per_device(
    genotypes, phenotypes, message, probes, inclusion, slab_ratio, input_precision, noise_precision
):
    people, markers = genotypes.shape
    zsize, group = lax.axis_size("sample"), lax.axis_size("marker")
    assert group == 2 * people // LANES and zsize == 4
    assert message.shape[0] == TRAITS and probes.shape[0] == ROWS - TRAITS
    chunks = max(1, people // 512)
    rest = ROWS - TRAITS
    quarter = markers // 8
    vmem = pltpu.VMEM
    dma = pltpu.SemaphoreType.DMA
    whole = pl.BlockSpec(memory_space=pltpu.VMEM)
    far = pl.BlockSpec(memory_space=pl.ANY)
    scalars = pl.BlockSpec(memory_space=pltpu.SMEM)
    out = jax.ShapeDtypeStruct((TRAITS, markers), F32)
    piece_t = vmem((group, 8, LANES), F32)
    piece_b = vmem((group, 8, LANES), BF16)
    piece_p = vmem((group, 64, LANES), BF16)
    trait_all = vmem((TRAITS, markers), F32)
    exact = vmem((2 * TRAITS, markers), F32)
    column = vmem((ROWS, 1), F32)
    centre, r0, back, coefs = pl.pallas_call(
        functools.partial(kernel, float(people * zsize), float(markers * group)),
        out_shape=(out, out, out, jax.ShapeDtypeStruct((TRAITS, LANES), F32)),
        in_specs=[far, far, far, far, scalars, scalars, scalars, scalars],
        out_specs=(whole, whole, whole, whole),
        scratch_shapes=[
            vmem((people, markers), BF16),
            vmem((TRAITS, people), F32),
            trait_all,
            vmem((rest, markers), F32),
            vmem((4 * TRAITS + rest, markers), BF16),
            vmem((TRAITS, markers), BF16),
            vmem((ROWS, markers), BF16),
            vmem((1, LANES), F32),
            vmem((group, 1, LANES), F32),
            vmem((4 * TRAITS, people), F32),
            piece_t,
            piece_t,
            vmem((8, LANES), BF16),
            piece_b,
            piece_p,
            piece_p,
            vmem((64, LANES), BF16),
            piece_p,
            piece_t,
            piece_t,
            vmem((8, LANES), BF16),
            piece_b,
            piece_p,
            piece_p,
            vmem((TRAITS, people), BF16),
            vmem((ROWS, people), BF16),
            vmem((ROWS, markers), F32),
            exact,
            exact,
            exact,
            exact,
            vmem((4, TRAITS, markers), BF16),
            vmem((4, TRAITS, markers), BF16),
            vmem((rest, markers), BF16),
            vmem((rest, 2 * quarter), BF16),
            vmem((rest, 2 * quarter), BF16),
            vmem((rest, quarter), BF16),
            vmem((rest, quarter), BF16),
            column,
            column,
            column,
            column,
            vmem((4, LANES), F32),
            vmem((group, 4, LANES), F32),
            vmem((4, LANES), F32),
            vmem((zsize, 4, LANES), F32),
            dma((chunks,)),
            dma((3,)),
            dma((9,)),
            dma((9,)),
            dma((chunks,)),
            dma((chunks,)),
            dma((20 + zsize,)),
            dma((20 + zsize,)),
        ],
        compiler_params=pltpu.CompilerParams(
            collective_id=0, has_side_effects=True, vmem_limit_bytes=56 << 20
        ),
        name="vamp_round",
    )(
        genotypes,
        phenotypes,
        message,
        probes,
        inclusion,
        slab_ratio,
        input_precision,
        noise_precision,
    )
    along_r, along_b, eta, prec, shrink, base = (coefs[:, k : k + 1] for k in range(6))
    lmmse = centre + along_r * r0 - along_b * back
    signal = (lmmse - eta * centre) / (1.0 - eta)
    return denoise(signal, prec, shrink, base)[0], lmmse


def solution(mesh):
    return jax.shard_map(
        per_device,
        mesh=mesh,
        in_specs=(
            P("sample", "marker"),
            P(None, "sample"),
            P(None, "marker"),
            P(None, "marker"),
            P(),
            P(),
            P(),
            P(),
        ),
        out_specs=(P(None, "marker"), P(None, "marker")),
        check_vma=False,
    )
```
